768 devices in a mesh: depth: 64 (over x, y, core), rows: 12 (over z).
Axes of the slice: x: 4, y: 8, z: 12, core: 2. Of those that a mesh axis runs over, the one named last changes fastest.
Arguments:
- density: float32 [512, 96, 1024], P('depth', 'rows'), may hold values from -6 to 6
- material: int32 [512, 96, 1024], P('depth', 'rows'), may hold values from 0 to 15
- absorption: float32 [16], replicated, may hold values from 0.5 to 4
- emission: float32 [8, 16], replicated, may hold values from 1 to 8
- shard_rank: int32 [64], replicated, may hold values from 0 to 63, each once
Outputs:
- smoothed: float32 [512, 96, 1024], P('depth', 'rows')
- band_image: float32 [8, 96, 1024], P(None, 'rows', 'depth')
- transmittance: float32 [96, 1024], P('rows', 'depth')
The draws below stay inside these ranges and needn't reach their ends.
Inputs may be any that keep to these rules, and one draw needn't show every extreme that they name: `shard_rank`: each value names one depth slab's rank, every rank once.
All inputs are finite; a program needn't handle non-finite values.
Results may differ from the reference program's by a relative error of at most 0.0003.
Values sent between devices are 32-bit elements; how exact they have to be, the bound alone decides.
A program may use at most 32 MiB of HBM per device.

```python
import math
import jax
import jax.numpy as jnp
from jax import lax

X = 1024
DZ = 8
SWEEPS = 4
BANDS = 8
CLASSES = 16
NZ = 512
NY = 96
N_DEPTH = 64


def plant(drawn, own_key, least, top_value):
    spot = [jax.random.randint(jax.random.fold_in(own_key, axis), (), 0, length) for axis, length in enumerate(drawn.shape)]
    main_axis = drawn.shape.index(max(drawn.shape))
    beside = spot[:main_axis] + [(spot[main_axis] + 1) % drawn.shape[main_axis]] + spot[main_axis + 1:]
    return drawn.at[tuple(spot)].set(least).at[tuple(beside)].set(top_value)


def block_levels(stream_key, extent, split, smallest, largest):
    loudness, own = 1.0, jax.random.fold_in(stream_key, 6)
    for position, blocks in split:
        draws = jnp.exp(jax.random.uniform(jax.random.fold_in(own, position), (blocks,), jnp.float32, smallest / len(split), largest / len(split)))
        loudness = loudness * jnp.repeat(draws, extent[position] // blocks).reshape([-1 if axis == position else 1 for axis in range(len(extent))])
    return loudness


def scatter_about(own_key, shape, width, limit, cuts=(), held_as=jnp.bfloat16):
    entries = jax.random.normal(own_key, shape, jnp.float32) * width
    if len(cuts) > 0:
        entries = block_levels(own_key, shape, cuts, -0.22, 0.18) * entries
    return jnp.clip(entries, min=-limit, max=limit).astype(held_as)


def setup_inputs(seed: int = 0) -> dict:
    splits = jax.random.split(jax.random.key(seed), 6)
    density = scatter_about(splits[0], (NZ, NY, X), 1.0, 6.0, ((0, 64), (1, 12)), jnp.float32)
    material = plant(jax.random.randint(splits[1], (NZ, NY, X), 0, CLASSES), jax.random.fold_in(splits[1], 1), 0, CLASSES - 1).astype(jnp.int32)
    absorption = jnp.clip(jnp.exp(jax.random.uniform(splits[2], (CLASSES,), jnp.float32, math.log(0.5), math.log(4.0))), 0.5, 4.0)
    emission = jnp.clip(jnp.exp(jax.random.uniform(splits[3], (BANDS, CLASSES), jnp.float32, math.log(1.0), math.log(8.0))), 1.0, 8.0)
    shard_rank = jax.random.permutation(splits[4], N_DEPTH).astype(jnp.int32)
    return dict(density=density, material=material, absorption=absorption, emission=emission, shard_rank=shard_rank)


time_step = 0.16
edge_scale = 1.5
light_z = 0.6
light_y = 0.48
light_x = 0.64
step_scale = 1.2

def conduct(diff):
    return diff / (1.0 + diff * diff * (1.0 / (edge_scale * edge_scale)))

def diffuse(padded):
    centre = padded[1:-1, 1:-1, 1:-1]
    total = conduct(padded[2:, 1:-1, 1:-1] - centre) + conduct(padded[:-2, 1:-1, 1:-1] - centre)
    total = total + conduct(padded[1:-1, 2:, 1:-1] - centre) + conduct(padded[1:-1, :-2, 1:-1] - centre)
    total = total + conduct(padded[1:-1, 1:-1, 2:] - centre) + conduct(padded[1:-1, 1:-1, :-2] - centre)
    return centre + time_step * total

def shading_of(padded):
    grad_z = (padded[2:, 1:-1, 1:-1] - padded[:-2, 1:-1, 1:-1]) * 0.5
    grad_y = (padded[1:-1, 2:, 1:-1] - padded[1:-1, :-2, 1:-1]) * 0.5
    grad_x = (padded[1:-1, 1:-1, 2:] - padded[1:-1, 1:-1, :-2]) * 0.5
    lambert = (grad_z * light_z + grad_y * light_y + grad_x * light_x) / jnp.sqrt(grad_z * grad_z + grad_y * grad_y + grad_x * grad_x + 1.0)
    return 0.55 + 0.45 * lambert

def reference(density, material, absorption, emission, shard_rank):
    field = density
    for sweep_index in range(SWEEPS):
        field = diffuse(jnp.pad(field, 1))
    shading = shading_of(jnp.pad(field, 1))
    step_len = step_scale / NZ
    optical = absorption[material] * jax.nn.softplus(field) * step_len
    opacity = 1.0 - jnp.exp(-optical)
    shape4 = (N_DEPTH, DZ, NY, X)
    optical4 = optical.reshape(shape4)
    inside = jnp.cumsum(optical4, axis=1) - optical4
    contrib = jnp.exp(-inside) * opacity.reshape(shape4) * shading.reshape(shape4)
    slab_depth = lax.optimization_barrier(jnp.sum(optical4, axis=1))
    material4 = material.reshape(shape4)
    ahead = (shard_rank[None, :] < shard_rank[:, None]).astype(jnp.float32)
    prior = jnp.einsum('tu,uyx->tyx', ahead, slab_depth, precision=lax.Precision.HIGHEST)
    weights = jnp.exp(-prior)
    planes = []
    for band in range(BANDS):
        slab_colour = lax.optimization_barrier(jnp.sum(contrib * emission[band][material4], axis=1))
        planes.append(lax.optimization_barrier(jnp.sum(weights * slab_colour, axis=0)))
    band_image = jnp.stack(planes)
    transmittance = jnp.exp(-lax.optimization_barrier(jnp.sum(slab_depth, axis=0)))
    return (field, band_image, transmittance)
```

```python
import functools

import jax
import jax.numpy as jnp
from jax import lax
from jax.experimental import pallas as pl
from jax.experimental.pallas import tpu as pltpu
from jax.sharding import PartitionSpec as P

MESH = pl.DeviceIdType.MESH
SWEEPS = 4
LANES = 128
SUB = 8

time_step = 0.16
edge_scale = 1.5
light_z = 0.6
light_y = 0.48
light_x = 0.64
step_scale = 1.2


def conduct(diff):
    return diff / (1.0 + diff * diff * (1.0 / (edge_scale * edge_scale)))


def roll(value, shift, axis):
    return pltpu.roll(value, shift % value.shape[axis], axis)


def gather(table, index):
    return jnp.take_along_axis(table, index, axis=1, mode="promise_in_bounds")


def kernel(
    n, n_rows, x_size,
    density, material, absorption, emission, rank,
    smoothed_out, band_out, trans_out,
    a0, a1, b0, b1, flux_a, flux_b, mat, face_z, face_y, pack_y, weight, tables, swap,
    colour_send, depth_send, colour_recv, depth_recv, slab_weight,
    local_sem, halo_send, halo_recv, face_send, face_recv, a2a_send, a2a_recv,
):
    slab, bands = SUB, emission.shape[0]
    tiles = x_size // LANES
    own = x_size // n
    group = LANES // own
    d = lax.axis_index("depth")
    r = lax.axis_index("rows")
    d_up, d_down = lax.rem(d + 1, n), lax.rem(d + n - 1, n)
    r_up, r_down = lax.rem(r + 1, n_rows), lax.rem(r + n_rows - 1, n_rows)

    local = [
        pltpu.make_async_copy(density, a0.at[4:12], local_sem.at[0]),
        pltpu.make_async_copy(material, mat, local_sem.at[1]),
    ]
    for copy in local:
        copy.start()

    barrier = pltpu.get_barrier_semaphore()

    @pl.loop(1, n)
    def _(i):
        pl.semaphore_signal(
            barrier, inc=1, device_id={"depth": lax.rem(d + i, n), "rows": r}, device_id_type=MESH
        )

    for dd in (d_down, d, d_up):
        for rr in (r_down, r_up):
            pl.semaphore_signal(barrier, inc=1, device_id={"depth": dd, "rows": rr}, device_id_type=MESH)
    pl.semaphore_wait(barrier, n - 1 + 6)

    parts = [
        (density.at[4:8], a0.at[0:4], d_up, r),
        (density.at[0:4], a0.at[12:16], d_down, r),
        (density.at[:, 0:4, :], b0.at[4:12, 0:4, :], d, r_down),
        (density.at[:, 4:8, :], b0.at[4:12, 4:8, :], d, r_up),
    ]
    for dd, source, target, step in ((d_up, 7, 3, -1), (d_down, 0, 12, 1)):
        for away in range(3):
            width = 3 - away
            low, high = slice(0, width), slice(SUB - width, SUB)
            parts.append((density.at[source + step * away, low, :], b0.at[target + step * away, low, :], dd, r_down))
            parts.append((density.at[source + step * away, high, :], b0.at[target + step * away, high, :], dd, r_up))
    halo = []
    for index, (source, target, dd, rr) in enumerate(parts):
        copy = pltpu.make_async_remote_copy(
            src_ref=source, dst_ref=target, send_sem=halo_send.at[index], recv_sem=halo_recv.at[index],
            device_id={"depth": dd, "rows": rr}, device_id_type=MESH,
        )
        copy.start()
        halo.append(copy)

    sub = lax.broadcasted_iota(jnp.int32, (SUB, LANES), 0)
    lane = lax.broadcasted_iota(jnp.int32, (SUB, LANES), 1)
    zero = jnp.zeros((SUB, LANES), jnp.float32)

    tables[...] = jnp.zeros_like(tables)
    entries = emission.shape[1]
    for band in range(bands):
        tables[band, :, 0:entries] = jnp.broadcast_to(emission[band : band + 1, :], (SUB, entries))
    tables[bands, :, 0:entries] = jnp.broadcast_to(absorption[...], (SUB, entries))

    for copy in local:
        copy.wait()
    for copy in halo:
        copy.wait()

    @pl.when(d == 0)
    def _():
        a0[0:4] = jnp.zeros((4, SUB, x_size), jnp.float32)
        b0[0:4] = jnp.zeros((4, SUB, x_size), jnp.float32)

    @pl.when(d == n - 1)
    def _():
        a0[12:16] = jnp.zeros((4, SUB, x_size), jnp.float32)
        b0[12:16] = jnp.zeros((4, SUB, x_size), jnp.float32)

    @pl.when(r == 0)
    def _():
        b0[:, 4:8, :] = jnp.zeros((16, 4, x_size), jnp.float32)

    @pl.when(r == n_rows - 1)
    def _():
        b0[:, 0:4, :] = jnp.zeros((16, 4, x_size), jnp.float32)

    coef_low = jnp.where(d > 0, time_step, 0.0)
    coef_high = jnp.where(d < n - 1, time_step, 0.0)
    keep_high_rows = jnp.where(r < n_rows - 1, 1.0, 0.0)
    keep_low_rows = jnp.where(r > 0, 1.0, 0.0)
    keep_b = jnp.where(sub < 4, keep_high_rows, keep_low_rows)

    def span(j):
        return slice(j * LANES, (j + 1) * LANES)

    def row_flux(values):
        fluxes = []
        for j in range(tiles):
            following = values[j + 1] if j + 1 < tiles else zero
            shifted = roll(jnp.where(lane == 0, following, values[j]), LANES - 1, 1)
            fluxes.append(conduct(shifted - values[j]))
        edge = conduct(values[0])
        change = []
        for j in range(tiles):
            before = roll(jnp.where(lane == LANES - 1, fluxes[j - 1], fluxes[j]), 1, 1) if j > 0 else jnp.where(
                lane == 0, edge, roll(fluxes[0], 1, 1)
            )
            change.append(fluxes[j] - before)
        return change

    def layer(z, src_a, src_b, dst_a, dst_b, with_b):
        coef = jnp.where(z < 4, coef_low, jnp.where(z >= 12, coef_high, time_step))
        va = [src_a[z, :, span(j)] for j in range(tiles)]
        vb = [src_b[z, :, span(j)] for j in range(tiles)]
        change = row_flux(va)
        change_b = row_flux(vb) if with_b else None
        for j in range(tiles):
            up_a = roll(jnp.where(sub == 0, vb[j], va[j]), SUB - 1, 0)
            y_a = conduct(up_a - va[j])
            z_a = conduct(src_a[z + 1, :, span(j)] - va[j])
            total_a = change[j] + (z_a - flux_a[:, span(j)])
            flux_a[:, span(j)] = z_a
            if with_b:
                up_b = roll(jnp.where(sub == 0, va[j], vb[j]), SUB - 1, 0)
                y_b = conduct(up_b - vb[j])
                z_b = conduct(src_b[z + 1, :, span(j)] - vb[j])
                total_b = change_b[j] + (z_b - flux_b[:, span(j)])
                flux_b[:, span(j)] = z_b
                total_a = total_a + (y_a - roll(jnp.where(sub == SUB - 1, y_b, y_a), 1, 0))
                total_b = total_b + (y_b - roll(jnp.where(sub == SUB - 1, y_a, y_b), 1, 0))
                dst_b[z, :, span(j)] = vb[j] + (coef * keep_b) * total_b
            else:
                down_a = roll(jnp.where(sub == SUB - 1, vb[j], va[j]), 1, 0)
                total_a = total_a + (y_a + conduct(down_a - va[j]))
            dst_a[z, :, span(j)] = va[j] + coef * total_a

    fields = ((a0, b0), (a1, b1))
    for sweep in range(SWEEPS):
        (src_a, src_b), (dst_a, dst_b) = fields[sweep % 2], fields[(sweep + 1) % 2]
        first, last = 1 + sweep, 14 - sweep
        for j in range(tiles):
            flux_a[:, span(j)] = conduct(src_a[first, :, span(j)] - src_a[first - 1, :, span(j)])
        if sweep + 1 < SWEEPS:
            for j in range(tiles):
                flux_b[:, span(j)] = conduct(src_b[first + 1, :, span(j)] - src_b[first, :, span(j)])
            layer(first, src_a, src_b, dst_a, dst_b, False)

            @pl.loop(first + 1, last)
            def _(z):
                layer(z, src_a, src_b, dst_a, dst_b, True)

            layer(last, src_a, src_b, dst_a, dst_b, False)
        else:

            @pl.loop(first, last + 1)
            def _(z):
                layer(z, src_a, src_b, dst_a, dst_b, False)

    result = pltpu.make_async_copy(a0.at[4:12], smoothed_out, local_sem.at[0])
    result.start()
    for z in range(slab):
        pack_y[0, z : z + 1, :] = a0[4 + z, 0:1, :]
        pack_y[1, z : z + 1, :] = a0[4 + z, SUB - 1 : SUB, :]
    faces = []
    for index, (source, target, dd, rr) in enumerate(
        (
            (a0.at[11], face_z.at[0], d_up, r),
            (a0.at[4], face_z.at[1], d_down, r),
            (pack_y.at[1], face_y.at[0], d, r_up),
            (pack_y.at[0], face_y.at[1], d, r_down),
        )
    ):
        copy = pltpu.make_async_remote_copy(
            src_ref=source, dst_ref=target, send_sem=face_send.at[index], recv_sem=face_recv.at[index],
            device_id={"depth": dd, "rows": rr}, device_id_type=MESH,
        )
        copy.start()
        faces.append(copy)

    step_len = step_scale / (slab * n)

    def lanes(j):
        return pl.ds(pl.multiple_of(j * LANES, LANES), LANES)

    @pl.loop(0, tiles)
    def _(j):
        at = lanes(j)
        depth = zero
        through = jnp.ones((SUB, LANES), jnp.float32)
        for k in range(slab):
            value = a0[4 + k, :, at]
            soft = jnp.maximum(value, 0.0) + jnp.log1p(jnp.exp(-jnp.abs(value)))
            depth = depth + gather(tables[bands], mat[k, :, at]) * soft * step_len
            after = jnp.exp(-depth)
            weight[k, :, at] = through - after
            through = after
        for t in (1, 2, 4):
            sub_bit = lax.rem(lax.div(sub, t), 2)
            lane_bit = lax.rem(lax.div(lane, own * t), 2)
            high = roll(roll(depth, t, 0), LANES - own * t, 1)
            low = roll(roll(depth, SUB - t, 0), own * t, 1)
            depth = jnp.where(sub_bit == lane_bit, depth, jnp.where(sub_bit == 1, high, low))
        depth_send[pl.ds(pl.multiple_of(j * group, group), group), 0, :] = depth

    def send(buffer, target_buffer, which, target):
        return pltpu.make_async_remote_copy(
            src_ref=buffer.at[target], dst_ref=target_buffer.at[d],
            send_sem=a2a_send.at[which], recv_sem=a2a_recv.at[which],
            device_id={"depth": target, "rows": r}, device_id_type=MESH,
        )

    @pl.loop(1, n)
    def _(i):
        send(depth_send, depth_recv, 0, lax.rem(d + i, n)).start()

    depth_recv[d] = depth_send[d]
    for copy in faces:
        copy.wait()

    @pl.when(d == 0)
    def _():
        face_z[0] = jnp.zeros((SUB, x_size), jnp.float32)

    @pl.when(d == n - 1)
    def _():
        face_z[1] = jnp.zeros((SUB, x_size), jnp.float32)

    @pl.when(r == 0)
    def _():
        face_y[0] = jnp.zeros((SUB, x_size), jnp.float32)

    @pl.when(r == n_rows - 1)
    def _():
        face_y[1] = jnp.zeros((SUB, x_size), jnp.float32)

    my_tile = lax.div(d, group)

    @pl.loop(0, tiles)
    def _(i):
        j = lax.rem(my_tile + i, tiles)
        at = lanes(j)
        at_left = lanes(jnp.maximum(j - 1, 0))
        at_right = lanes(jnp.minimum(j + 1, tiles - 1))
        has_left = jnp.where(j > 0, 1.0, 0.0)
        has_right = jnp.where(j < tiles - 1, 1.0, 0.0)
        colour = [zero] * bands
        for k in range(slab):
            value = a0[4 + k, :, at]
            right = roll(jnp.where(lane == 0, a0[4 + k, :, at_right] * has_right, value), LANES - 1, 1)
            left = roll(jnp.where(lane == LANES - 1, a0[4 + k, :, at_left] * has_left, value), 1, 1)
            above = roll(jnp.where(sub == 0, face_y[1, k : k + 1, at], value), SUB - 1, 0)
            below = roll(jnp.where(sub == SUB - 1, face_y[0, k : k + 1, at], value), 1, 0)
            deeper = a0[5 + k, :, at] if k + 1 < slab else face_z[1, :, at]
            nearer = a0[3 + k, :, at] if k > 0 else face_z[0, :, at]
            grad_z = (deeper - nearer) * 0.5
            grad_y = (above - below) * 0.5
            grad_x = (right - left) * 0.5
            lambert = (grad_z * light_z + grad_y * light_y + grad_x * light_x) * lax.rsqrt(
                grad_z * grad_z + grad_y * grad_y + grad_x * grad_x + 1.0
            )
            contrib = weight[k, :, at] * (0.55 + 0.45 * lambert)
            ids = mat[k, :, at]
            for band in range(bands):
                colour[band] = colour[band] + contrib * gather(tables[band], ids)
        for band in range(bands):
            swap[pl.ds(band, SUB, stride=bands), :] = colour[band]
        planes = [swap[y * bands : (y + 1) * bands, :] for y in range(SUB)]
        for t in (1, 2, 4):
            lane_bit = lax.rem(lax.div(lane, own * t), 2) == 0
            updated = list(planes)
            for y in range(SUB):
                if y & t:
                    continue
                low, high = planes[y], planes[y | t]
                updated[y] = jnp.where(lane_bit, low, roll(high, own * t, 1))
                updated[y | t] = jnp.where(lane_bit, roll(low, LANES - own * t, 1), high)
            planes = updated
        for o in range(group):
            colour_send[j * group + o] = planes[o]
        for o in range(group):
            target = j * group + lax.rem(d + o, group)

            @pl.when(target != d)
            def _():
                send(colour_send, colour_recv, 1, target).start()

    colour_recv[d] = colour_send[d]

    def all_of(ref, which):
        return pltpu.make_async_remote_copy(
            src_ref=ref.at[pl.ds(0, n - 1)], dst_ref=ref.at[pl.ds(0, n - 1)],
            send_sem=a2a_send.at[which], recv_sem=a2a_recv.at[which],
            device_id={"depth": d_up, "rows": r}, device_id_type=MESH,
        )

    all_of(depth_recv, 0).wait_recv()
    row_rank = jnp.broadcast_to(rank[...].astype(jnp.float32), (n, n))
    diagonal = lax.broadcasted_iota(jnp.int32, (n, n), 0) == lax.broadcasted_iota(jnp.int32, (n, n), 1)
    column_rank = jnp.sum(jnp.where(diagonal, row_rank, 0.0), axis=1, keepdims=True)
    ahead = jnp.where(row_rank < column_rank, 1.0, 0.0)
    depths = depth_recv[:, 0, :]
    prior = jnp.dot(ahead, depths, precision=lax.Precision.HIGHEST, preferred_element_type=jnp.float32)
    slab_weight[...] = jnp.exp(-prior)
    trans_out[...] = jnp.exp(-jnp.sum(depths, axis=0, keepdims=True))

    all_of(colour_recv, 1).wait_recv()
    total = [zero] * 4
    for s in range(n):
        total[s % 4] = total[s % 4] + slab_weight[s : s + 1, :] * colour_recv[s]
    band_out[...] = (total[0] + total[1]) + (total[2] + total[3])

    all_of(depth_send, 0).wait_send()
    all_of(colour_send, 1).wait_send()
    result.wait()


def solution(mesh):
    n, n_rows = mesh.shape["depth"], mesh.shape["rows"]

    def body(density, material, absorption, emission, shard_rank):
        slab, row_count, x_size = density.shape
        bands, classes = emission.shape
        own = x_size // n
        vmem = pl.BlockSpec(memory_space=pltpu.VMEM)
        hbm = pl.BlockSpec(memory_space=pl.ANY)
        f32 = functools.partial(pltpu.VMEM, dtype=jnp.float32)
        dma = pltpu.SemaphoreType.DMA
        smoothed, band, trans = pl.pallas_call(
            functools.partial(kernel, n, n_rows, x_size),
            out_shape=(
                jax.ShapeDtypeStruct(density.shape, jnp.float32),
                jax.ShapeDtypeStruct((bands, LANES), jnp.float32),
                jax.ShapeDtypeStruct((1, LANES), jnp.float32),
            ),
            in_specs=[hbm, hbm, vmem, vmem, vmem],
            out_specs=(hbm, vmem, vmem),
            scratch_shapes=[
                f32((16, SUB, x_size)), f32((16, SUB, x_size)), f32((16, SUB, x_size)), f32((16, SUB, x_size)),
                f32((SUB, x_size)), f32((SUB, x_size)),
                pltpu.VMEM(material.shape, jnp.int32),
                f32((2, SUB, x_size)), f32((2, SUB, x_size)), f32((2, SUB, x_size)),
                f32(density.shape),
                f32((bands + 1, SUB, LANES)),
                f32((SUB * bands, LANES)),
                f32((n, bands, LANES)), f32((n, 1, LANES)), f32((n, bands, LANES)), f32((n, 1, LANES)),
                f32((n, LANES)),
                dma((2,)), dma((16,)), dma((16,)), dma((4,)), dma((4,)), dma((2,)), dma((2,)),
            ],
            compiler_params=pltpu.CompilerParams(collective_id=0, has_side_effects=True),
        )(density, material, absorption.reshape(1, classes), emission, shard_rank.reshape(1, n))
        return (
            smoothed,
            band.reshape(bands, row_count, own),
            trans.reshape(row_count, own),
        )

    in_specs = (P("depth", "rows", None), P("depth", "rows", None), P(), P(), P())
    out_specs = (P("depth", "rows", None), P(None, "rows", "depth"), P("rows", "depth"))
    return jax.shard_map(body, mesh=mesh, in_specs=in_specs, out_specs=out_specs, check_vma=False)
```

```python
import functools

import jax
import jax.numpy as jnp
from jax import lax
from jax.experimental import pallas as pl
from jax.experimental.pallas import tpu as pltpu
from jax.sharding import PartitionSpec as P

MESH = pl.DeviceIdType.MESH
SWEEPS = 4
LANES = 128
SUB = 8
UNROLL = 2
CHIPS_X, CHIPS_Y = 4, 8

time_step = 0.16
edge_scale = 1.5
light_z = 0.6
light_y = 0.48
light_x = 0.64
step_scale = 1.2


def flux(diff):
    return diff / (edge_scale * edge_scale + diff * diff)


def roll(value, shift, axis):
    return pltpu.roll(value, shift % value.shape[axis], axis)


def gather(table, index):
    return jnp.take_along_axis(table, index, axis=1, mode="promise_in_bounds")


def kernel(
    n, n_rows, x_size,
    density, material, absorption, emission, rank,
    smooth, band_out, trans_out,
    a0, a1, b0, b1, flux_a, flux_b, mat, face_z, face_y, pack_y, weight, tables, swap,
    outbox, inbox, slab_weight,
    local_sem, halo_send, halo_recv, face_send, face_recv, a2a_send, a2a_recv, token,
):
    slab, bands = SUB, emission.shape[0]
    tiles = x_size // LANES
    own = x_size // n
    group = LANES // own
    d = lax.axis_index("depth")
    r = lax.axis_index("rows")
    has_depth = {-1: d > 0, 0: None, 1: d < n - 1}
    has_rows = {-1: r > 0, 0: None, 1: r < n_rows - 1}

    def exists(dd, rr):
        conditions = [c for c in (has_depth[dd], has_rows[rr]) if c is not None]
        return functools.reduce(jnp.logical_and, conditions)

    def to(dd, rr):
        return {"depth": d + dd, "rows": r + rr}

    def signal(sem, device):
        pl.semaphore_signal(sem, inc=1, device_id=device, device_id_type=MESH)

    core = lax.rem(d, 2)
    chip_y = lax.rem(lax.div(d, 2), CHIPS_Y)
    chip_x = lax.div(d, 2 * CHIPS_Y)

    def chip(dx, dy, other):
        x = lax.rem(chip_x + (dx + CHIPS_X), CHIPS_X)
        y = lax.rem(chip_y + (dy + CHIPS_Y), CHIPS_Y)
        return {"depth": (x * CHIPS_Y + y) * 2 + (1 - core if other else core), "rows": r}

    barrier = pltpu.get_barrier_semaphore()
    for dd in (-1, 0, 1):
        for rr in (-1, 1):
            pl.when(exists(dd, rr))(functools.partial(signal, barrier, to(dd, rr)))
    close = [
        (dx, dy, other) for dx in (-1, 0, 1) for dy in (-1, 0, 1) for other in (0, 1) if (dx, dy, other) != (0, 0, 0)
    ]
    for offset in close:
        signal(barrier, chip(*offset))

    local = [
        pltpu.make_async_copy(density, a0.at[4:12], local_sem.at[0]),
        pltpu.make_async_copy(material, mat, local_sem.at[1]),
    ]
    for copy in local:
        copy.start()

    def count(conditions):
        return sum(jnp.where(c, 1, 0) for c in conditions)

    beside = count((has_rows[-1], has_rows[1])) * (1 + count((has_depth[-1], has_depth[1])))
    pl.semaphore_wait(barrier, len(close) + beside)

    stages = [[(dx, dy, 0) for dx in (-1, 1) for dy in (-1, 1)], [(0, -2, 0), (0, 2, 0)]]

    def spread(stage):
        if stage > 0:
            for index in range(len(stages[stage - 1])):
                pl.semaphore_wait(token.at[stage - 1, index], 1)
        if stage < len(stages):
            for index, offset in enumerate(stages[stage]):
                signal(token.at[stage, index], chip(*offset))

    def exchange(parts, send_sem, recv_sem):
        copies = []
        for index, (source, target, dd, rr) in enumerate(parts):
            copy = pltpu.make_async_remote_copy(
                src_ref=source, dst_ref=target, send_sem=send_sem.at[index], recv_sem=recv_sem.at[index],
                device_id=to(dd, rr), device_id_type=MESH,
            )
            pl.when(exists(dd, rr))(copy.start)
            copies.append((copy, exists(dd, rr), exists(-dd, -rr)))
        return copies

    def finish(copies):
        for copy, _, arrives in copies:
            pl.when(arrives)(copy.wait_recv)

    def drain(copies):
        for copy, leaves, _ in copies:
            pl.when(leaves)(copy.wait_send)

    parts = [
        (density.at[:, 0:4, :], b0.at[4:12, 0:4, :], 0, -1),
        (density.at[:, 4:8, :], b0.at[4:12, 4:8, :], 0, 1),
        (density.at[4:8], a0.at[0:4], 1, 0),
        (density.at[0:4], a0.at[12:16], -1, 0),
    ]
    for dd, source, target, step in ((1, 7, 3, -1), (-1, 0, 12, 1)):
        for away in range(3):
            width = 3 - away
            low, high = slice(0, width), slice(SUB - width, SUB)
            parts.append((density.at[source + step * away, low, :], b0.at[target + step * away, low, :], dd, -1))
            parts.append((density.at[source + step * away, high, :], b0.at[target + step * away, high, :], dd, 1))
    halo = exchange(parts, halo_send, halo_recv)
    spread(0)

    sub = lax.broadcasted_iota(jnp.int32, (SUB, LANES), 0)
    lane = lax.broadcasted_iota(jnp.int32, (SUB, LANES), 1)
    zero = jnp.zeros((SUB, LANES), jnp.float32)

    tables[...] = jnp.zeros_like(tables)
    entries = emission.shape[1]
    for band in range(bands):
        tables[band, :, 0:entries] = jnp.broadcast_to(emission[band : band + 1, :], (SUB, entries))
    tables[bands, :, 0:entries] = jnp.broadcast_to(absorption[...], (SUB, entries))

    for copy in local:
        copy.wait()
    finish(halo)
    spread(1)

    @pl.when(d == 0)
    def _():
        a0[0:4] = jnp.zeros((4, SUB, x_size), jnp.float32)
        b0[0:4] = jnp.zeros((4, SUB, x_size), jnp.float32)

    @pl.when(d == n - 1)
    def _():
        a0[12:16] = jnp.zeros((4, SUB, x_size), jnp.float32)
        b0[12:16] = jnp.zeros((4, SUB, x_size), jnp.float32)

    @pl.when(r == 0)
    def _():
        b0[:, 4:8, :] = jnp.zeros((16, 4, x_size), jnp.float32)

    @pl.when(r == n_rows - 1)
    def _():
        b0[:, 0:4, :] = jnp.zeros((16, 4, x_size), jnp.float32)

    scale = time_step * edge_scale * edge_scale
    coef_low = jnp.where(d > 0, scale, 0.0)
    coef_high = jnp.where(d < n - 1, scale, 0.0)
    keep_high_rows = jnp.where(r < n_rows - 1, 1.0, 0.0)
    keep_low_rows = jnp.where(r > 0, 1.0, 0.0)
    keep_b = jnp.where(sub < 4, keep_high_rows, keep_low_rows)

    def span(j):
        return slice(j * LANES, (j + 1) * LANES)

    def along_row(value, following, before):
        shifted = roll(jnp.where(lane == 0, following, value), LANES - 1, 1)
        out = flux(shifted - value)
        if before is None:
            back = jnp.where(lane == 0, flux(value), roll(out, 1, 1))
        else:
            back = roll(jnp.where(lane == LANES - 1, before, out), 1, 1)
        return out, out - back

    def layer(z, src_a, src_b, dst_a, dst_b, with_b, offset=0):
        coef = jnp.where(z < 4, coef_low, jnp.where(z >= 12, coef_high, scale))
        x_a = x_b = None
        for j in range(tiles):
            here, beyond = span(j), span(j + 1)
            a, b = src_a[z, :, here], src_b[z, :, here]
            x_a, total_a = along_row(a, src_a[z, :, beyond] if j + 1 < tiles else zero, x_a)
            z_a = flux(src_a[z + 1, :, here] - a)
            total_a = total_a + (z_a - flux_a[:, here])
            flux_a[:, here] = z_a
            y_a = flux(roll(jnp.where(sub == 0, b, a), SUB - 1, 0) - a)
            if with_b:
                x_b, total_b = along_row(b, src_b[z, :, beyond] if j + 1 < tiles else zero, x_b)
                z_b = flux(src_b[z + 1, :, here] - b)
                total_b = total_b + (z_b - flux_b[:, here])
                flux_b[:, here] = z_b
                y_b = flux(roll(jnp.where(sub == 0, a, b), SUB - 1, 0) - b)
                total_a = total_a + (y_a - roll(jnp.where(sub == SUB - 1, y_b, y_a), 1, 0))
                total_b = total_b + (y_b - roll(jnp.where(sub == SUB - 1, y_a, y_b), 1, 0))
                dst_b[z, :, here] = b + (coef * keep_b) * total_b
            else:
                total_a = total_a + (y_a + flux(roll(jnp.where(sub == SUB - 1, b, a), 1, 0) - a))
            dst_a[z - offset, :, here] = a + coef * total_a

    fields = ((a0, b0), (a1, b1))
    for sweep in range(SWEEPS):
        (src_a, src_b), (dst_a, dst_b) = fields[sweep % 2], fields[(sweep + 1) % 2]
        first, last = 1 + sweep, 14 - sweep
        for j in range(tiles):
            flux_a[:, span(j)] = flux(src_a[first, :, span(j)] - src_a[first - 1, :, span(j)])
        if sweep + 1 < SWEEPS:
            for j in range(tiles):
                flux_b[:, span(j)] = flux(src_b[first + 1, :, span(j)] - src_b[first, :, span(j)])
            layer(first, src_a, src_b, dst_a, dst_b, False)

            @pl.loop(0, last - first - 1, unroll=UNROLL)
            def _(i):
                layer(first + 1 + i, src_a, src_b, dst_a, dst_b, True)

            layer(last, src_a, src_b, dst_a, dst_b, False)
        else:

            @pl.loop(0, last + 1 - first, unroll=UNROLL)
            def _(i):
                layer(first + i, src_a, src_b, smooth, None, False, 4)

    for z in range(slab):
        pack_y[0, z : z + 1, :] = smooth[z, 0:1, :]
        pack_y[1, z : z + 1, :] = smooth[z, SUB - 1 : SUB, :]
    faces = exchange(
        (
            (pack_y.at[1], face_y.at[0], 0, 1),
            (pack_y.at[0], face_y.at[1], 0, -1),
            (smooth.at[slab - 1], face_z.at[0], 1, 0),
            (smooth.at[0], face_z.at[1], -1, 0),
        ),
        face_send, face_recv,
    )

    step_len = step_scale / (slab * n)

    def lanes(j):
        return pl.ds(pl.multiple_of(j * LANES, LANES), LANES)

    @pl.loop(0, tiles)
    def _(j):
        at = lanes(j)
        depth = zero
        through = jnp.ones((SUB, LANES), jnp.float32)
        for k in range(slab):
            value = smooth[k, :, at]
            soft = jnp.maximum(value, 0.0) + jnp.log1p(jnp.exp(-jnp.abs(value)))
            depth = depth + gather(tables[bands], mat[k, :, at]) * soft * step_len
            after = jnp.exp(-depth)
            weight[k, :, at] = through - after
            through = after
        for t in (1, 2, 4):
            sub_bit = lax.rem(lax.div(sub, t), 2)
            lane_bit = lax.rem(lax.div(lane, own * t), 2)
            high = roll(roll(depth, t, 0), LANES - own * t, 1)
            low = roll(roll(depth, SUB - t, 0), own * t, 1)
            depth = jnp.where(sub_bit == lane_bit, depth, jnp.where(sub_bit == 1, high, low))
        outbox[pl.ds(pl.multiple_of(j * group, group), group), bands, :] = depth

    spread(2)
    finish(faces)

    @pl.when(d == 0)
    def _():
        face_z[0] = jnp.zeros((SUB, x_size), jnp.float32)

    @pl.when(d == n - 1)
    def _():
        face_z[1] = jnp.zeros((SUB, x_size), jnp.float32)

    @pl.when(r == 0)
    def _():
        face_y[0] = jnp.zeros((SUB, x_size), jnp.float32)

    @pl.when(r == n_rows - 1)
    def _():
        face_y[1] = jnp.zeros((SUB, x_size), jnp.float32)

    my_tile = lax.div(d, group)

    def tile_of(i):
        return lax.rem(my_tile + 1 + i, tiles)

    def post(i, first):
        for o in range(first, group):
            target = tile_of(i) * group + lax.rem(d + o, group)
            pltpu.make_async_remote_copy(
                src_ref=outbox.at[target], dst_ref=inbox.at[d], send_sem=a2a_send, recv_sem=a2a_recv,
                device_id={"depth": target, "rows": r}, device_id_type=MESH,
            ).start()

    def shade(i):
        j = tile_of(i)
        at = lanes(j)
        at_left = lanes(jnp.maximum(j - 1, 0))
        at_right = lanes(jnp.minimum(j + 1, tiles - 1))
        has_left = jnp.where(j > 0, 1.0, 0.0)
        has_right = jnp.where(j < tiles - 1, 1.0, 0.0)
        colour = [zero] * bands
        for k in range(slab):
            value = smooth[k, :, at]
            right = roll(jnp.where(lane == 0, smooth[k, :, at_right] * has_right, value), LANES - 1, 1)
            left = roll(jnp.where(lane == LANES - 1, smooth[k, :, at_left] * has_left, value), 1, 1)
            above = roll(jnp.where(sub == 0, face_y[1, k : k + 1, at], value), SUB - 1, 0)
            below = roll(jnp.where(sub == SUB - 1, face_y[0, k : k + 1, at], value), 1, 0)
            deeper = smooth[k + 1, :, at] if k + 1 < slab else face_z[1, :, at]
            nearer = smooth[k - 1, :, at] if k > 0 else face_z[0, :, at]
            grad_z = (deeper - nearer) * 0.5
            grad_y = (above - below) * 0.5
            grad_x = (right - left) * 0.5
            lambert = (grad_z * light_z + grad_y * light_y + grad_x * light_x) * lax.rsqrt(
                grad_z * grad_z + grad_y * grad_y + grad_x * grad_x + 1.0
            )
            contrib = weight[k, :, at] * (0.55 + 0.45 * lambert)
            ids = mat[k, :, at]
            for band in range(bands):
                colour[band] = colour[band] + contrib * gather(tables[band], ids)
        for band in range(bands):
            swap[pl.ds(band, SUB, stride=bands), :] = colour[band]
        planes = [swap[y * bands : (y + 1) * bands, :] for y in range(SUB)]
        for t in (1, 2, 4):
            lane_bit = lax.rem(lax.div(lane, own * t), 2) == 0
            updated = list(planes)
            for y in range(SUB):
                if y & t:
                    continue
                low, high = planes[y], planes[y | t]
                updated[y] = jnp.where(lane_bit, low, roll(high, own * t, 1))
                updated[y | t] = jnp.where(lane_bit, roll(low, LANES - own * t, 1), high)
            planes = updated
        for o in range(group):
            outbox[j * group + o, 0:bands, :] = planes[o]

    shade(0)

    @pl.loop(1, tiles)
    def _(i):
        post(i - 1, 0)
        shade(i)

    post(tiles - 1, 1)
    inbox[d] = outbox[d]

    def all_of(ref):
        return pltpu.make_async_remote_copy(
            src_ref=ref.at[pl.ds(0, n - 1)], dst_ref=ref.at[pl.ds(0, n - 1)], send_sem=a2a_send, recv_sem=a2a_recv,
            device_id=chip(0, 0, 1), device_id_type=MESH,
        )

    all_of(inbox).wait_recv()
    row_rank = jnp.broadcast_to(rank[...].astype(jnp.float32), (n, n))
    diagonal = lax.broadcasted_iota(jnp.int32, (n, n), 0) == lax.broadcasted_iota(jnp.int32, (n, n), 1)
    column_rank = jnp.sum(jnp.where(diagonal, row_rank, 0.0), axis=1, keepdims=True)
    ahead = jnp.where(row_rank < column_rank, 1.0, 0.0)
    depths = inbox[:, bands, :]
    prior = jnp.dot(ahead, depths, precision=lax.Precision.HIGHEST, preferred_element_type=jnp.float32)
    slab_weight[...] = jnp.exp(-prior)
    trans_out[...] = jnp.exp(-jnp.sum(depths, axis=0, keepdims=True))

    total = [zero] * 4
    for s in range(n):
        total[s % 4] = total[s % 4] + slab_weight[s : s + 1, :] * inbox[s, 0:bands, :]
    band_out[...] = (total[0] + total[1]) + (total[2] + total[3])

    drain(halo)
    drain(faces)
    all_of(outbox).wait_send()


def place(own, smooth, band, trans, smoothed_out, band_out, trans_out, sem):
    outward = pltpu.make_async_copy(smooth, smoothed_out, sem)
    outward.start()
    for y in range(SUB):
        lanes = slice(y * own, (y + 1) * own)
        for b in range(band.shape[0]):
            band_out[b, y : y + 1, :] = band[b : b + 1, lanes]
        trans_out[y : y + 1, :] = trans[:, lanes]
    outward.wait()


def solution(mesh):
    n, n_rows = mesh.shape["depth"], mesh.shape["rows"]

    def body(density, material, absorption, emission, shard_rank):
        slab, row_count, x_size = density.shape
        bands, classes = emission.shape
        own = x_size // n
        vmem = pl.BlockSpec(memory_space=pltpu.VMEM)
        hbm = pl.BlockSpec(memory_space=pl.ANY)
        f32 = functools.partial(pltpu.VMEM, dtype=jnp.float32)
        dma = pltpu.SemaphoreType.DMA
        smoothed, band, trans = pl.pallas_call(
            functools.partial(kernel, n, n_rows, x_size),
            out_shape=(f32(density.shape), f32((bands, LANES)), f32((1, LANES))),
            in_specs=[hbm, hbm, vmem, vmem, vmem],
            out_specs=(vmem, vmem, vmem),
            scratch_shapes=[
                f32((16, SUB, x_size)), f32((16, SUB, x_size)), f32((16, SUB, x_size)), f32((16, SUB, x_size)),
                f32((SUB, x_size)), f32((SUB, x_size)),
                pltpu.VMEM(material.shape, jnp.int32),
                f32((2, SUB, x_size)), f32((2, SUB, x_size)), f32((2, SUB, x_size)),
                f32(density.shape),
                f32((bands + 1, SUB, LANES)),
                f32((SUB * bands, LANES)),
                f32((n, bands + 1, LANES)), f32((n, bands + 1, LANES)),
                f32((n, LANES)),
                dma((2,)), dma((16,)), dma((16,)), dma((4,)), dma((4,)), dma, dma, pltpu.SemaphoreType.REGULAR((2, 4)),
            ],
            compiler_params=pltpu.CompilerParams(collective_id=0, has_side_effects=True),
        )(density, material, absorption.reshape(1, classes), emission, shard_rank.reshape(1, n))
        return pl.pallas_call(
            functools.partial(place, own),
            out_shape=(
                jax.ShapeDtypeStruct(density.shape, jnp.float32),
                jax.ShapeDtypeStruct((bands, row_count, own), jnp.float32),
                jax.ShapeDtypeStruct((row_count, own), jnp.float32),
            ),
            in_specs=[vmem, vmem, vmem],
            out_specs=(hbm, vmem, vmem),
            scratch_shapes=[dma],
        )(*(pltpu.with_memory_space_constraint(x, pltpu.VMEM) for x in (smoothed, band, trans)))

    in_specs = (P("depth", "rows", None), P("depth", "rows", None), P(), P(), P())
    out_specs = (P("depth", "rows", None), P(None, "rows", "depth"), P("rows", "depth"))
    return jax.shard_map(body, mesh=mesh, in_specs=in_specs, out_specs=out_specs, check_vma=False)
```

```python
import functools

import jax
import jax.numpy as jnp
from jax import lax
from jax.experimental import pallas as pl
from jax.experimental.pallas import tpu as pltpu
from jax.sharding import PartitionSpec as P

MESH = pl.DeviceIdType.MESH
SWEEPS = 4
LANES = 128
SUB = 8
UNROLL = 2
CHIPS_X, CHIPS_Y = 4, 8

time_step = 0.16
edge_scale = 1.5
light_z = 0.6
light_y = 0.48
light_x = 0.64
step_scale = 1.2


def flux(diff):
    return diff / (edge_scale * edge_scale + diff * diff)


def roll(value, shift, axis):
    return pltpu.roll(value, shift % value.shape[axis], axis)


def gather(table, index):
    return jnp.take_along_axis(table, index, axis=1, mode="promise_in_bounds")


def kernel(
    n, n_rows, x_size,
    density, material, absorption_in, emission_in, rank_in,
    smooth, band_out, trans_out,
    a0, a1, b0, b1, flux_a, flux_b, mat, face_z, face_y, pack_y, weight, tables, swap,
    outbox, inbox, slab_weight, absorption, emission, rank, ahead,
    local_sem, halo_send, halo_recv, face_send, face_recv, a2a_send, a2a_recv, token,
):
    slab, bands = SUB, emission.shape[0]
    tiles = x_size // LANES
    own = x_size // n
    group = LANES // own
    d = lax.axis_index("depth")
    r = lax.axis_index("rows")
    has_depth = {-1: d > 0, 0: None, 1: d < n - 1}
    has_rows = {-1: r > 0, 0: None, 1: r < n_rows - 1}

    def exists(dd, rr):
        conditions = [c for c in (has_depth[dd], has_rows[rr]) if c is not None]
        return functools.reduce(jnp.logical_and, conditions)

    def to(dd, rr):
        return {"depth": d + dd, "rows": r + rr}

    def signal(sem, device):
        pl.semaphore_signal(sem, inc=1, device_id=device, device_id_type=MESH)

    core = lax.rem(d, 2)
    chip_y = lax.rem(lax.div(d, 2), CHIPS_Y)
    chip_x = lax.div(d, 2 * CHIPS_Y)

    def chip(dx, dy, other):
        x = lax.rem(chip_x + (dx + CHIPS_X), CHIPS_X)
        y = lax.rem(chip_y + (dy + CHIPS_Y), CHIPS_Y)
        return {"depth": (x * CHIPS_Y + y) * 2 + (1 - core if other else core), "rows": r}

    barrier = pltpu.get_barrier_semaphore()
    for dd in (-1, 0, 1):
        for rr in (-1, 1):
            pl.when(exists(dd, rr))(functools.partial(signal, barrier, to(dd, rr)))
    close = [
        (dx, dy, other) for dx in (-1, 0, 1) for dy in (-1, 0, 1) for other in (0, 1) if (dx, dy, other) != (0, 0, 0)
    ]
    for offset in close:
        signal(barrier, chip(*offset))

    local = [
        pltpu.make_async_copy(density, a0.at[4:12], local_sem.at[0]),
        pltpu.make_async_copy(emission_in, emission, local_sem.at[1]),
        pltpu.make_async_copy(absorption_in, absorption, local_sem.at[2]),
        pltpu.make_async_copy(rank_in, rank, local_sem.at[3]),
        pltpu.make_async_copy(material, mat, local_sem.at[4]),
    ]
    for copy in local:
        copy.start()

    def count(conditions):
        return sum(jnp.where(c, 1, 0) for c in conditions)

    beside = count((has_rows[-1], has_rows[1])) * (1 + count((has_depth[-1], has_depth[1])))
    pl.semaphore_wait(barrier, len(close) + beside)

    stages = [[(dx, dy, 0) for dx in (-1, 1) for dy in (-1, 1)], [(0, -2, 0), (0, 2, 0)]]

    def spread(stage):
        if stage > 0:
            for index in range(len(stages[stage - 1])):
                pl.semaphore_wait(token.at[stage - 1, index], 1)
        if stage < len(stages):
            for index, offset in enumerate(stages[stage]):
                signal(token.at[stage, index], chip(*offset))

    def exchange(parts, send_sem, recv_sem, base=0):
        copies = []
        for index, (source, target, dd, rr) in enumerate(parts):
            copy = pltpu.make_async_remote_copy(
                src_ref=source, dst_ref=target, send_sem=send_sem.at[base + index], recv_sem=recv_sem.at[base + index],
                device_id=to(dd, rr), device_id_type=MESH,
            )
            pl.when(exists(dd, rr))(copy.start)
            copies.append((copy, exists(dd, rr), exists(-dd, -rr)))
        return copies

    def finish(copies):
        for copy, _, arrives in copies:
            pl.when(arrives)(copy.wait_recv)

    def drain(copies):
        for copy, leaves, _ in copies:
            pl.when(leaves)(copy.wait_send)

    parts = [
        (density.at[:, 0:4, :], b0.at[4:12, 0:4, :], 0, -1),
        (density.at[:, 4:8, :], b0.at[4:12, 4:8, :], 0, 1),
        (density.at[4:8], a0.at[0:4], 1, 0),
        (density.at[0:4], a0.at[12:16], -1, 0),
    ]
    for dd, source, target, step in ((1, 7, 3, -1), (-1, 0, 12, 1)):
        for away in range(3):
            width = 3 - away
            low, high = slice(0, width), slice(SUB - width, SUB)
            parts.append((density.at[source + step * away, low, :], b0.at[target + step * away, low, :], dd, -1))
            parts.append((density.at[source + step * away, high, :], b0.at[target + step * away, high, :], dd, 1))
    halo = exchange(parts, halo_send, halo_recv)
    beside_halo, corner_halo = halo[:4], halo[4:]
    spread(0)

    sub = lax.broadcasted_iota(jnp.int32, (SUB, LANES), 0)
    lane = lax.broadcasted_iota(jnp.int32, (SUB, LANES), 1)
    zero = jnp.zeros((SUB, LANES), jnp.float32)

    for copy in local:
        copy.wait()
    tables[...] = jnp.zeros_like(tables)
    entries = emission.shape[1]
    for band in range(bands):
        tables[band, :, 0:entries] = jnp.broadcast_to(emission[band : band + 1, :], (SUB, entries))
    tables[bands, :, 0:entries] = jnp.broadcast_to(absorption[...], (SUB, entries))

    @pl.when(d == 0)
    def _():
        a0[0:4] = jnp.zeros((4, SUB, x_size), jnp.float32)
        b0[0:4] = jnp.zeros((4, SUB, x_size), jnp.float32)

    @pl.when(d == n - 1)
    def _():
        a0[12:16] = jnp.zeros((4, SUB, x_size), jnp.float32)
        b0[12:16] = jnp.zeros((4, SUB, x_size), jnp.float32)

    @pl.when(r == 0)
    def _():
        b0[:, 4:8, :] = jnp.zeros((16, 4, x_size), jnp.float32)

    @pl.when(r == n_rows - 1)
    def _():
        b0[:, 0:4, :] = jnp.zeros((16, 4, x_size), jnp.float32)

    @pl.when(d == 0)
    def _():
        face_z[0] = jnp.zeros((SUB, x_size), jnp.float32)

    @pl.when(d == n - 1)
    def _():
        face_z[1] = jnp.zeros((SUB, x_size), jnp.float32)

    @pl.when(r == 0)
    def _():
        face_y[0] = jnp.zeros((SUB, x_size), jnp.float32)

    @pl.when(r == n_rows - 1)
    def _():
        face_y[1] = jnp.zeros((SUB, x_size), jnp.float32)

    row_rank = jnp.broadcast_to(rank[...].astype(jnp.float32), (n, n))
    diagonal = lax.broadcasted_iota(jnp.int32, (n, n), 0) == lax.broadcasted_iota(jnp.int32, (n, n), 1)
    column_rank = jnp.sum(jnp.where(diagonal, row_rank, 0.0), axis=1, keepdims=True)
    ahead[...] = jnp.where(row_rank < column_rank, 1.0, 0.0)
    spread(1)
    finish(beside_halo)

    scale = time_step * edge_scale * edge_scale
    coef_low = jnp.where(d > 0, scale, 0.0)
    coef_high = jnp.where(d < n - 1, scale, 0.0)
    keep_high_rows = jnp.where(r < n_rows - 1, 1.0, 0.0)
    keep_low_rows = jnp.where(r > 0, 1.0, 0.0)
    keep_b = jnp.where(sub < 4, keep_high_rows, keep_low_rows)

    def span(j):
        return slice(j * LANES, (j + 1) * LANES)

    def along_row(value, following, before):
        shifted = roll(jnp.where(lane == 0, following, value), LANES - 1, 1)
        out = flux(shifted - value)
        if before is None:
            back = jnp.where(lane == 0, flux(value), roll(out, 1, 1))
        else:
            back = roll(jnp.where(lane == LANES - 1, before, out), 1, 1)
        return out, out - back

    def layer(z, src_a, src_b, dst_a, dst_b, with_b, offset=0):
        coef = jnp.where(z < 4, coef_low, jnp.where(z >= 12, coef_high, scale))
        x_a = x_b = None
        for j in range(tiles):
            here, beyond = span(j), span(j + 1)
            a, b = src_a[z, :, here], src_b[z, :, here]
            x_a, total_a = along_row(a, src_a[z, :, beyond] if j + 1 < tiles else zero, x_a)
            z_a = flux(src_a[z + 1, :, here] - a)
            total_a = total_a + (z_a - flux_a[:, here])
            flux_a[:, here] = z_a
            y_a = flux(roll(jnp.where(sub == 0, b, a), SUB - 1, 0) - a)
            if with_b:
                x_b, total_b = along_row(b, src_b[z, :, beyond] if j + 1 < tiles else zero, x_b)
                z_b = flux(src_b[z + 1, :, here] - b)
                total_b = total_b + (z_b - flux_b[:, here])
                flux_b[:, here] = z_b
                y_b = flux(roll(jnp.where(sub == 0, a, b), SUB - 1, 0) - b)
                total_a = total_a + (y_a - roll(jnp.where(sub == SUB - 1, y_b, y_a), 1, 0))
                total_b = total_b + (y_b - roll(jnp.where(sub == SUB - 1, y_a, y_b), 1, 0))
                dst_b[z, :, here] = b + (coef * keep_b) * total_b
            else:
                total_a = total_a + (y_a + flux(roll(jnp.where(sub == SUB - 1, b, a), 1, 0) - a))
            dst_a[z - offset, :, here] = a + coef * total_a

    fields = ((a0, b0), (a1, b1))
    for sweep in range(SWEEPS):
        (src_a, src_b), (dst_a, dst_b) = fields[sweep % 2], fields[(sweep + 1) % 2]
        first, last = 1 + sweep, 14 - sweep

        def start(z, with_a=True, with_b=True):
            for j in range(tiles):
                if with_a:
                    flux_a[:, span(j)] = flux(src_a[z, :, span(j)] - src_a[z - 1, :, span(j)])
                if with_b:
                    flux_b[:, span(j)] = flux(src_b[z, :, span(j)] - src_b[z - 1, :, span(j)])

        def both(z):
            layer(z, src_a, src_b, dst_a, dst_b, True)

        def only_a(z):
            layer(z, src_a, src_b, dst_a, dst_b, False)

        if sweep == 0:
            start(5)

            @pl.loop(0, slab - 2, unroll=UNROLL)
            def _(i):
                both(5 + i)

            finish(corner_halo)
            for z in (11, 12, 13):
                both(z)
            only_a(14)
            start(1, with_b=False)
            start(2, with_a=False)
            for z in (1, 2, 3, 4):
                (only_a if z == 1 else both)(z)
            drain(halo)
        elif sweep + 1 < SWEEPS:
            start(first, with_b=False)
            start(first + 1, with_a=False)
            only_a(first)

            @pl.loop(0, last - first - 1, unroll=UNROLL)
            def _(i):
                both(first + 1 + i)

            only_a(last)
        else:
            def final(z):
                layer(z, src_a, src_b, smooth, None, False, 4)

            start(last, with_b=False)
            final(last)
            start(first, with_b=False)
            final(first)
            deep_faces = exchange(
                ((smooth.at[slab - 1], face_z.at[0], 1, 0), (smooth.at[0], face_z.at[1], -1, 0)), face_send, face_recv
            )

            @pl.loop(1, last - first, unroll=UNROLL)
            def _(i):
                final(first + i)

    for z in range(slab):
        pack_y[0, z : z + 1, :] = smooth[z, 0:1, :]
        pack_y[1, z : z + 1, :] = smooth[z, SUB - 1 : SUB, :]
    faces = deep_faces + exchange(
        ((pack_y.at[1], face_y.at[0], 0, 1), (pack_y.at[0], face_y.at[1], 0, -1)), face_send, face_recv, 2
    )

    step_len = step_scale / (slab * n)

    def lanes(j):
        return pl.ds(pl.multiple_of(j * LANES, LANES), LANES)

    @pl.loop(0, tiles, unroll=UNROLL)
    def _(j):
        at = lanes(j)
        depth = zero
        through = jnp.ones((SUB, LANES), jnp.float32)
        for k in range(slab):
            value = smooth[k, :, at]
            soft = jnp.maximum(value, 0.0) + jnp.log1p(jnp.exp(-jnp.abs(value)))
            depth = depth + gather(tables[bands], mat[k, :, at]) * soft * step_len
            after = jnp.exp(-depth)
            weight[k, :, at] = through - after
            through = after
        for t in (1, 2, 4):
            sub_bit = lax.rem(lax.div(sub, t), 2)
            lane_bit = lax.rem(lax.div(lane, own * t), 2)
            high = roll(roll(depth, t, 0), LANES - own * t, 1)
            low = roll(roll(depth, SUB - t, 0), own * t, 1)
            depth = jnp.where(sub_bit == lane_bit, depth, jnp.where(sub_bit == 1, high, low))
        outbox[pl.ds(pl.multiple_of(j * group, group), group), bands, :] = depth

    finish(faces)

    my_tile = lax.div(d, group)

    order = [5, 3, 4, 7, 1, 2, 6, 0]

    def tile_of(i):
        return i

    def post(i, first):
        for o in range(first, group):
            target = tile_of(i) * group + lax.rem(d + o, group)
            pl.when(target != d)(pltpu.make_async_remote_copy(
                src_ref=outbox.at[target], dst_ref=inbox.at[d], send_sem=a2a_send, recv_sem=a2a_recv,
                device_id={"depth": target, "rows": r}, device_id_type=MESH,
            ).start)

    def shade(i):
        j = tile_of(i)
        at = lanes(j)
        at_left = lanes(jnp.maximum(j - 1, 0))
        at_right = lanes(jnp.minimum(j + 1, tiles - 1))
        has_left = jnp.where(j > 0, 1.0, 0.0)
        has_right = jnp.where(j < tiles - 1, 1.0, 0.0)
        colour = [zero] * bands
        for k in range(slab):
            value = smooth[k, :, at]
            right = roll(jnp.where(lane == 0, smooth[k, :, at_right] * has_right, value), LANES - 1, 1)
            left = roll(jnp.where(lane == LANES - 1, smooth[k, :, at_left] * has_left, value), 1, 1)
            above = roll(jnp.where(sub == 0, face_y[1, k : k + 1, at], value), SUB - 1, 0)
            below = roll(jnp.where(sub == SUB - 1, face_y[0, k : k + 1, at], value), 1, 0)
            deeper = smooth[k + 1, :, at] if k + 1 < slab else face_z[1, :, at]
            nearer = smooth[k - 1, :, at] if k > 0 else face_z[0, :, at]
            grad_z = (deeper - nearer) * 0.5
            grad_y = (above - below) * 0.5
            grad_x = (right - left) * 0.5
            lambert = (grad_z * light_z + grad_y * light_y + grad_x * light_x) * lax.rsqrt(
                grad_z * grad_z + grad_y * grad_y + grad_x * grad_x + 1.0
            )
            contrib = weight[k, :, at] * (0.55 + 0.45 * lambert)
            ids = mat[k, :, at]
            for band in range(bands):
                colour[band] = colour[band] + contrib * gather(tables[band], ids)
        for band in range(bands):
            swap[i % 2, pl.ds(band, SUB, stride=bands), :] = colour[band]
        planes = [swap[i % 2, y * bands : (y + 1) * bands, :] for y in range(SUB)]
        for t in (1, 2, 4):
            lane_bit = lax.rem(lax.div(lane, own * t), 2) == 0
            updated = list(planes)
            for y in range(SUB):
                if y & t:
                    continue
                low, high = planes[y], planes[y | t]
                updated[y] = jnp.where(lane_bit, low, roll(high, own * t, 1))
                updated[y | t] = jnp.where(lane_bit, roll(low, LANES - own * t, 1), high)
            planes = updated
        for o in range(group):
            outbox[j * group + o, 0:bands, :] = planes[o]

    for i in range(tiles):
        if i == 2:
            spread(2)
        if i % 2 == 0 and i > 0:
            post(i - 2, 0)
            post(i - 1, 0)
        shade(i)
    post(tiles - 2, 0)
    post(tiles - 1, 0)
    inbox[d] = outbox[d]

    def all_of(ref):
        return pltpu.make_async_remote_copy(
            src_ref=ref.at[pl.ds(0, n - 1)], dst_ref=ref.at[pl.ds(0, n - 1)], send_sem=a2a_send, recv_sem=a2a_recv,
            device_id=chip(0, 0, 1), device_id_type=MESH,
        )

    all_of(inbox).wait_recv()
    depths = inbox[:, bands, :]
    prior = jnp.dot(ahead[...], depths, precision=lax.Precision.HIGHEST, preferred_element_type=jnp.float32)
    slab_weight[...] = jnp.exp(-prior)
    trans_out[...] = jnp.exp(-jnp.sum(depths, axis=0, keepdims=True))

    total = [zero] * 4
    for s in range(n):
        total[s % 4] = total[s % 4] + slab_weight[s : s + 1, :] * inbox[s, 0:bands, :]
    band_out[...] = (total[0] + total[1]) + (total[2] + total[3])

    drain(faces)
    all_of(outbox).wait_send()


def place(own, smooth, band, trans, smoothed_out, band_out, trans_out, sem):
    outward = pltpu.make_async_copy(smooth, smoothed_out, sem)
    outward.start()
    for y in range(SUB):
        lanes = slice(y * own, (y + 1) * own)
        for b in range(band.shape[0]):
            band_out[b, y : y + 1, :] = band[b : b + 1, lanes]
        trans_out[y : y + 1, :] = trans[:, lanes]
    outward.wait()


def solution(mesh):
    n, n_rows = mesh.shape["depth"], mesh.shape["rows"]

    def body(density, material, absorption, emission, shard_rank):
        slab, row_count, x_size = density.shape
        bands, classes = emission.shape
        own = x_size // n
        vmem = pl.BlockSpec(memory_space=pltpu.VMEM)
        hbm = pl.BlockSpec(memory_space=pl.ANY)
        f32 = functools.partial(pltpu.VMEM, dtype=jnp.float32)
        dma = pltpu.SemaphoreType.DMA
        smoothed, band, trans = pl.pallas_call(
            functools.partial(kernel, n, n_rows, x_size),
            out_shape=(f32(density.shape), f32((bands, LANES)), f32((1, LANES))),
            in_specs=[hbm, hbm, hbm, hbm, hbm],
            out_specs=(vmem, vmem, vmem),
            scratch_shapes=[
                f32((16, SUB, x_size)), f32((16, SUB, x_size)), f32((16, SUB, x_size)), f32((16, SUB, x_size)),
                f32((SUB, x_size)), f32((SUB, x_size)),
                pltpu.VMEM(material.shape, jnp.int32),
                f32((2, SUB, x_size)), f32((2, SUB, x_size)), f32((2, SUB, x_size)),
                f32(density.shape),
                f32((bands + 1, SUB, LANES)),
                f32((2, SUB * bands, LANES)),
                f32((n, bands + 1, LANES)), f32((n, bands + 1, LANES)),
                f32((n, LANES)), f32((1, classes)), f32((bands, classes)), pltpu.VMEM((1, n), jnp.int32), f32((n, n)),
                dma((5,)), dma((16,)), dma((16,)), dma((4,)), dma((4,)), dma, dma, pltpu.SemaphoreType.REGULAR((2, 4)),
            ],
            compiler_params=pltpu.CompilerParams(collective_id=0, has_side_effects=True),
        )(density, material, absorption.reshape(1, classes), emission, shard_rank.reshape(1, n))
        return pl.pallas_call(
            functools.partial(place, own),
            out_shape=(
                jax.ShapeDtypeStruct(density.shape, jnp.float32),
                jax.ShapeDtypeStruct((bands, row_count, own), jnp.float32),
                jax.ShapeDtypeStruct((row_count, own), jnp.float32),
            ),
            in_specs=[vmem, vmem, vmem],
            out_specs=(hbm, vmem, vmem),
            scratch_shapes=[dma],
        )(*(pltpu.with_memory_space_constraint(x, pltpu.VMEM) for x in (smoothed, band, trans)))

    in_specs = (P("depth", "rows", None), P("depth", "rows", None), P(), P(), P())
    out_specs = (P("depth", "rows", None), P(None, "rows", "depth"), P("rows", "depth"))
    return jax.shard_map(body, mesh=mesh, in_specs=in_specs, out_specs=out_specs, check_vma=False)
```

```python
import functools

import jax
import jax.numpy as jnp
from jax import lax
from jax.experimental import pallas as pl
from jax.experimental.pallas import tpu as pltpu
from jax.sharding import PartitionSpec as P

MESH = pl.DeviceIdType.MESH
SWEEPS = 4
LANES = 128
SUB = 8
UNROLL = 2
CHIPS_X, CHIPS_Y = 4, 8

time_step = 0.16
edge_scale = 1.5
light_z = 0.6
light_y = 0.48
light_x = 0.64
step_scale = 1.2


def flux(diff):
    return diff / (edge_scale * edge_scale + diff * diff)


def roll(value, shift, axis):
    return pltpu.roll(value, shift % value.shape[axis], axis)


def gather(table, index):
    return jnp.take_along_axis(table, index, axis=1, mode="promise_in_bounds")


def kernel(
    n, n_rows, x_size,
    density, material, absorption_in, emission_in, rank_in,
    smooth, band_out, trans_out,
    a0, a1, b0, b1, flux_a, flux_b, mat, face_z, face_y, pack_y, weight, tables, swap,
    outbox, inbox, slab_weight, absorption, emission, rank, ahead,
    local_sem, halo_send, halo_recv, face_send, face_recv, a2a_send, a2a_recv, token,
):
    slab, bands = SUB, emission.shape[0]
    tiles = x_size // LANES
    own = x_size // n
    group = LANES // own
    d = lax.axis_index("depth")
    r = lax.axis_index("rows")
    has_depth = {-1: d > 0, 0: None, 1: d < n - 1}
    has_rows = {-1: r > 0, 0: None, 1: r < n_rows - 1}

    def exists(dd, rr):
        conditions = [c for c in (has_depth[dd], has_rows[rr]) if c is not None]
        return functools.reduce(jnp.logical_and, conditions)

    def to(dd, rr):
        return {"depth": d + dd, "rows": r + rr}

    def signal(sem, device):
        pl.semaphore_signal(sem, inc=1, device_id=device, device_id_type=MESH)

    core = lax.rem(d, 2)
    chip_y = lax.rem(lax.div(d, 2), CHIPS_Y)
    chip_x = lax.div(d, 2 * CHIPS_Y)

    def chip(dx, dy, other):
        x = lax.rem(chip_x + (dx + CHIPS_X), CHIPS_X)
        y = lax.rem(chip_y + (dy + CHIPS_Y), CHIPS_Y)
        return {"depth": (x * CHIPS_Y + y) * 2 + (1 - core if other else core), "rows": r}

    barrier = pltpu.get_barrier_semaphore()
    for dd in (-1, 0, 1):
        for rr in (-1, 1):
            pl.when(exists(dd, rr))(functools.partial(signal, barrier, to(dd, rr)))
    close = [
        (dx, dy, other) for dx in (-1, 0, 1) for dy in (-1, 0, 1) for other in (0, 1) if (dx, dy, other) != (0, 0, 0)
    ]
    for offset in close:
        signal(barrier, chip(*offset))

    local = [
        pltpu.make_async_copy(density, a0.at[4:12], local_sem.at[0]),
        pltpu.make_async_copy(emission_in, emission, local_sem.at[1]),
        pltpu.make_async_copy(absorption_in, absorption, local_sem.at[2]),
        pltpu.make_async_copy(rank_in, rank, local_sem.at[3]),
        pltpu.make_async_copy(material, mat, local_sem.at[4]),
    ]
    for copy in local:
        copy.start()

    def count(conditions):
        return sum(jnp.where(c, 1, 0) for c in conditions)

    beside = count((has_rows[-1], has_rows[1])) * (1 + count((has_depth[-1], has_depth[1])))
    pl.semaphore_wait(barrier, len(close) + beside)

    stages = [[(dx, dy, 0) for dx in (-1, 1) for dy in (-1, 1)], [(0, -2, 0), (0, 2, 0)]]

    def spread(stage):
        if stage > 0:
            for index in range(len(stages[stage - 1])):
                pl.semaphore_wait(token.at[stage - 1, index], 1)
        if stage < len(stages):
            for index, offset in enumerate(stages[stage]):
                signal(token.at[stage, index], chip(*offset))

    def exchange(parts, send_sem, recv_sem, base=0):
        copies = []
        for index, (source, target, dd, rr) in enumerate(parts):
            copy = pltpu.make_async_remote_copy(
                src_ref=source, dst_ref=target, send_sem=send_sem.at[base + index], recv_sem=recv_sem.at[base + index],
                device_id=to(dd, rr), device_id_type=MESH,
            )
            pl.when(exists(dd, rr))(copy.start)
            copies.append((copy, exists(dd, rr), exists(-dd, -rr)))
        return copies

    def finish(copies):
        for copy, _, arrives in copies:
            pl.when(arrives)(copy.wait_recv)

    def drain(copies):
        for copy, leaves, _ in copies:
            pl.when(leaves)(copy.wait_send)

    parts = [
        (density.at[:, 0:4, :], b0.at[4:12, 0:4, :], 0, -1),
        (density.at[:, 4:8, :], b0.at[4:12, 4:8, :], 0, 1),
        (density.at[4:8], a0.at[0:4], 1, 0),
        (density.at[0:4], a0.at[12:16], -1, 0),
    ]
    for dd, source, target, step in ((1, 7, 3, -1), (-1, 0, 12, 1)):
        for away in range(3):
            width = 3 - away
            low, high = slice(0, width), slice(SUB - width, SUB)
            parts.append((density.at[source + step * away, low, :], b0.at[target + step * away, low, :], dd, -1))
            parts.append((density.at[source + step * away, high, :], b0.at[target + step * away, high, :], dd, 1))
    halo = exchange(parts, halo_send, halo_recv)
    beside_halo, corner_halo = halo[:4], halo[4:]
    spread(0)

    sub = lax.broadcasted_iota(jnp.int32, (SUB, LANES), 0)
    lane = lax.broadcasted_iota(jnp.int32, (SUB, LANES), 1)
    zero = jnp.zeros((SUB, LANES), jnp.float32)

    for copy in local:
        copy.wait()
    tables[...] = jnp.zeros_like(tables)
    entries = emission.shape[1]
    for band in range(bands):
        tables[band, :, 0:entries] = jnp.broadcast_to(emission[band : band + 1, :], (SUB, entries))
    tables[bands, :, 0:entries] = jnp.broadcast_to(absorption[...], (SUB, entries))

    @pl.when(d == 0)
    def _():
        a0[0:4] = jnp.zeros((4, SUB, x_size), jnp.float32)
        b0[0:4] = jnp.zeros((4, SUB, x_size), jnp.float32)

    @pl.when(d == n - 1)
    def _():
        a0[12:16] = jnp.zeros((4, SUB, x_size), jnp.float32)
        b0[12:16] = jnp.zeros((4, SUB, x_size), jnp.float32)

    @pl.when(r == 0)
    def _():
        b0[:, 4:8, :] = jnp.zeros((16, 4, x_size), jnp.float32)

    @pl.when(r == n_rows - 1)
    def _():
        b0[:, 0:4, :] = jnp.zeros((16, 4, x_size), jnp.float32)

    @pl.when(d == 0)
    def _():
        face_z[0] = jnp.zeros((SUB, x_size), jnp.float32)

    @pl.when(d == n - 1)
    def _():
        face_z[1] = jnp.zeros((SUB, x_size), jnp.float32)

    @pl.when(r == 0)
    def _():
        face_y[0] = jnp.zeros((SUB, x_size), jnp.float32)

    @pl.when(r == n_rows - 1)
    def _():
        face_y[1] = jnp.zeros((SUB, x_size), jnp.float32)

    row_rank = jnp.broadcast_to(rank[...].astype(jnp.float32), (n, n))
    diagonal = lax.broadcasted_iota(jnp.int32, (n, n), 0) == lax.broadcasted_iota(jnp.int32, (n, n), 1)
    column_rank = jnp.sum(jnp.where(diagonal, row_rank, 0.0), axis=1, keepdims=True)
    ahead[...] = jnp.where(row_rank < column_rank, 1.0, 0.0)
    spread(1)
    finish(beside_halo)

    scale = time_step * edge_scale * edge_scale
    coef_low = jnp.where(d > 0, scale, 0.0)
    coef_high = jnp.where(d < n - 1, scale, 0.0)
    keep_high_rows = jnp.where(r < n_rows - 1, 1.0, 0.0)
    keep_low_rows = jnp.where(r > 0, 1.0, 0.0)
    keep_b = jnp.where(sub < 4, keep_high_rows, keep_low_rows)

    def span(j):
        return slice(j * LANES, (j + 1) * LANES)

    def along_row(value, following, before):
        shifted = roll(jnp.where(lane == 0, following, value), LANES - 1, 1)
        out = flux(shifted - value)
        if before is None:
            back = jnp.where(lane == 0, flux(value), roll(out, 1, 1))
        else:
            back = roll(jnp.where(lane == LANES - 1, before, out), 1, 1)
        return out, out - back

    def layer(z, src_a, src_b, dst_a, dst_b, with_b, offset=0):
        coef = jnp.where(z < 4, coef_low, jnp.where(z >= 12, coef_high, scale))
        x_a = x_b = None
        for j in range(tiles):
            here, beyond = span(j), span(j + 1)
            a, b = src_a[z, :, here], src_b[z, :, here]
            x_a, total_a = along_row(a, src_a[z, :, beyond] if j + 1 < tiles else zero, x_a)
            z_a = flux(src_a[z + 1, :, here] - a)
            total_a = total_a + (z_a - flux_a[:, here])
            flux_a[:, here] = z_a
            y_a = flux(roll(jnp.where(sub == 0, b, a), SUB - 1, 0) - a)
            if with_b:
                x_b, total_b = along_row(b, src_b[z, :, beyond] if j + 1 < tiles else zero, x_b)
                z_b = flux(src_b[z + 1, :, here] - b)
                total_b = total_b + (z_b - flux_b[:, here])
                flux_b[:, here] = z_b
                y_b = flux(roll(jnp.where(sub == 0, a, b), SUB - 1, 0) - b)
                total_a = total_a + (y_a - roll(jnp.where(sub == SUB - 1, y_b, y_a), 1, 0))
                total_b = total_b + (y_b - roll(jnp.where(sub == SUB - 1, y_a, y_b), 1, 0))
                dst_b[z, :, here] = b + (coef * keep_b) * total_b
            else:
                total_a = total_a + (y_a + flux(roll(jnp.where(sub == SUB - 1, b, a), 1, 0) - a))
            dst_a[z - offset, :, here] = a + coef * total_a

    fields = ((a0, b0), (a1, b1))
    for sweep in range(SWEEPS):
        (src_a, src_b), (dst_a, dst_b) = fields[sweep % 2], fields[(sweep + 1) % 2]
        first, last = 1 + sweep, 14 - sweep

        def start(z, with_a=True, with_b=True):
            for j in range(tiles):
                if with_a:
                    flux_a[:, span(j)] = flux(src_a[z, :, span(j)] - src_a[z - 1, :, span(j)])
                if with_b:
                    flux_b[:, span(j)] = flux(src_b[z, :, span(j)] - src_b[z - 1, :, span(j)])

        def both(z):
            layer(z, src_a, src_b, dst_a, dst_b, True)

        def only_a(z):
            layer(z, src_a, src_b, dst_a, dst_b, False)

        if sweep == 0:
            start(5)

            @pl.loop(0, slab - 2, unroll=3)
            def _(i):
                both(5 + i)

            finish(corner_halo)
            for z in (11, 12, 13):
                both(z)
            only_a(14)
            start(1, with_b=False)
            start(2, with_a=False)
            for z in (1, 2, 3, 4):
                (only_a if z == 1 else both)(z)
            drain(halo)
        elif sweep + 1 < SWEEPS:
            start(first, with_b=False)
            start(first + 1, with_a=False)
            only_a(first)

            @pl.loop(0, last - first - 1, unroll=5 if (last - first - 1) % 5 == 0 else 4)
            def _(i):
                both(first + 1 + i)

            only_a(last)
        else:
            def final(z):
                layer(z, src_a, src_b, smooth, None, False, 4)

            start(last, with_b=False)
            final(last)
            start(first, with_b=False)
            final(first)
            deep_faces = exchange(
                ((smooth.at[slab - 1], face_z.at[0], 1, 0), (smooth.at[0], face_z.at[1], -1, 0)), face_send, face_recv
            )

            @pl.loop(1, last - first, unroll=3)
            def _(i):
                final(first + i)

    for z in range(slab):
        pack_y[0, z : z + 1, :] = smooth[z, 0:1, :]
        pack_y[1, z : z + 1, :] = smooth[z, SUB - 1 : SUB, :]
    faces = deep_faces + exchange(
        ((pack_y.at[1], face_y.at[0], 0, 1), (pack_y.at[0], face_y.at[1], 0, -1)), face_send, face_recv, 2
    )

    step_len = step_scale / (slab * n)

    def lanes(j):
        return pl.ds(pl.multiple_of(j * LANES, LANES), LANES)

    @pl.loop(0, tiles, unroll=4)
    def _(j):
        at = lanes(j)
        depth = zero
        through = jnp.ones((SUB, LANES), jnp.float32)
        for k in range(slab):
            value = smooth[k, :, at]
            soft = jnp.maximum(value, 0.0) + jnp.log1p(jnp.exp(-jnp.abs(value)))
            depth = depth + gather(tables[bands], mat[k, :, at]) * soft * step_len
            after = jnp.exp(-depth)
            weight[k, :, at] = through - after
            through = after
        for t in (1, 2, 4):
            sub_bit = lax.rem(lax.div(sub, t), 2)
            lane_bit = lax.rem(lax.div(lane, own * t), 2)
            high = roll(roll(depth, t, 0), LANES - own * t, 1)
            low = roll(roll(depth, SUB - t, 0), own * t, 1)
            depth = jnp.where(sub_bit == lane_bit, depth, jnp.where(sub_bit == 1, high, low))
        outbox[pl.ds(pl.multiple_of(j * group, group), group), bands, :] = depth

    finish(faces)

    my_tile = lax.div(d, group)

    order = [5, 3, 4, 7, 1, 2, 6, 0]

    def tile_of(i):
        return i

    def post(i, first):
        for o in range(first, group):
            target = tile_of(i) * group + lax.rem(d + o, group)
            pl.when(target != d)(pltpu.make_async_remote_copy(
                src_ref=outbox.at[target], dst_ref=inbox.at[d], send_sem=a2a_send, recv_sem=a2a_recv,
                device_id={"depth": target, "rows": r}, device_id_type=MESH,
            ).start)

    def shade(i):
        j = tile_of(i)
        at = lanes(j)
        at_left = lanes(jnp.maximum(j - 1, 0))
        at_right = lanes(jnp.minimum(j + 1, tiles - 1))
        has_left = jnp.where(j > 0, 1.0, 0.0)
        has_right = jnp.where(j < tiles - 1, 1.0, 0.0)
        colour = [zero] * bands
        for k in range(slab):
            value = smooth[k, :, at]
            right = roll(jnp.where(lane == 0, smooth[k, :, at_right] * has_right, value), LANES - 1, 1)
            left = roll(jnp.where(lane == LANES - 1, smooth[k, :, at_left] * has_left, value), 1, 1)
            above = roll(jnp.where(sub == 0, face_y[1, k : k + 1, at], value), SUB - 1, 0)
            below = roll(jnp.where(sub == SUB - 1, face_y[0, k : k + 1, at], value), 1, 0)
            deeper = smooth[k + 1, :, at] if k + 1 < slab else face_z[1, :, at]
            nearer = smooth[k - 1, :, at] if k > 0 else face_z[0, :, at]
            grad_z = (deeper - nearer) * 0.5
            grad_y = (above - below) * 0.5
            grad_x = (right - left) * 0.5
            lambert = (grad_z * light_z + grad_y * light_y + grad_x * light_x) * lax.rsqrt(
                grad_z * grad_z + grad_y * grad_y + grad_x * grad_x + 1.0
            )
            contrib = weight[k, :, at] * (0.55 + 0.45 * lambert)
            ids = mat[k, :, at]
            for band in range(bands):
                colour[band] = colour[band] + contrib * gather(tables[band], ids)
        for band in range(bands):
            swap[i % 2, pl.ds(band, SUB, stride=bands), :] = colour[band]
        planes = [swap[i % 2, y * bands : (y + 1) * bands, :] for y in range(SUB)]
        for t in (1, 2, 4):
            lane_bit = lax.rem(lax.div(lane, own * t), 2) == 0
            updated = list(planes)
            for y in range(SUB):
                if y & t:
                    continue
                low, high = planes[y], planes[y | t]
                updated[y] = jnp.where(lane_bit, low, roll(high, own * t, 1))
                updated[y | t] = jnp.where(lane_bit, roll(low, LANES - own * t, 1), high)
            planes = updated
        for o in range(group):
            outbox[j * group + o, 0:bands, :] = planes[o]

    for i in range(tiles):
        if i == 2:
            spread(2)
        if i % 2 == 0 and i > 0:
            post(i - 2, 0)
            post(i - 1, 0)
        shade(i)
    post(tiles - 2, 0)
    post(tiles - 1, 0)
    inbox[d] = outbox[d]

    def all_of(ref):
        return pltpu.make_async_remote_copy(
            src_ref=ref.at[pl.ds(0, n - 1)], dst_ref=ref.at[pl.ds(0, n - 1)], send_sem=a2a_send, recv_sem=a2a_recv,
            device_id=chip(0, 0, 1), device_id_type=MESH,
        )

    all_of(inbox).wait_recv()
    depths = inbox[:, bands, :]
    prior = jnp.dot(ahead[...], depths, precision=lax.Precision.HIGHEST, preferred_element_type=jnp.float32)
    slab_weight[...] = jnp.exp(-prior)
    trans_out[...] = jnp.exp(-jnp.sum(depths, axis=0, keepdims=True))

    total = [zero] * 4
    for s in range(n):
        total[s % 4] = total[s % 4] + slab_weight[s : s + 1, :] * inbox[s, 0:bands, :]
    band_out[...] = (total[0] + total[1]) + (total[2] + total[3])

    drain(faces)
    all_of(outbox).wait_send()


def place(own, smooth, band, trans, smoothed_out, band_out, trans_out, sem):
    outward = pltpu.make_async_copy(smooth, smoothed_out, sem)
    outward.start()
    for y in range(SUB):
        lanes = slice(y * own, (y + 1) * own)
        for b in range(band.shape[0]):
            band_out[b, y : y + 1, :] = band[b : b + 1, lanes]
        trans_out[y : y + 1, :] = trans[:, lanes]
    outward.wait()


def solution(mesh):
    n, n_rows = mesh.shape["depth"], mesh.shape["rows"]

    def body(density, material, absorption, emission, shard_rank):
        slab, row_count, x_size = density.shape
        bands, classes = emission.shape
        own = x_size // n
        vmem = pl.BlockSpec(memory_space=pltpu.VMEM)
        hbm = pl.BlockSpec(memory_space=pl.ANY)
        f32 = functools.partial(pltpu.VMEM, dtype=jnp.float32)
        dma = pltpu.SemaphoreType.DMA
        smoothed, band, trans = pl.pallas_call(
            functools.partial(kernel, n, n_rows, x_size),
            out_shape=(f32(density.shape), f32((bands, LANES)), f32((1, LANES))),
            in_specs=[hbm, hbm, hbm, hbm, hbm],
            out_specs=(vmem, vmem, vmem),
            scratch_shapes=[
                f32((16, SUB, x_size)), f32((16, SUB, x_size)), f32((16, SUB, x_size)), f32((16, SUB, x_size)),
                f32((SUB, x_size)), f32((SUB, x_size)),
                pltpu.VMEM(material.shape, jnp.int32),
                f32((2, SUB, x_size)), f32((2, SUB, x_size)), f32((2, SUB, x_size)),
                f32(density.shape),
                f32((bands + 1, SUB, LANES)),
                f32((2, SUB * bands, LANES)),
                f32((n, bands + 1, LANES)), f32((n, bands + 1, LANES)),
                f32((n, LANES)), f32((1, classes)), f32((bands, classes)), pltpu.VMEM((1, n), jnp.int32), f32((n, n)),
                dma((5,)), dma((16,)), dma((16,)), dma((4,)), dma((4,)), dma, dma, pltpu.SemaphoreType.REGULAR((2, 4)),
            ],
            compiler_params=pltpu.CompilerParams(collective_id=0, has_side_effects=True),
        )(density, material, absorption.reshape(1, classes), emission, shard_rank.reshape(1, n))
        return pl.pallas_call(
            functools.partial(place, own),
            out_shape=(
                jax.ShapeDtypeStruct(density.shape, jnp.float32),
                jax.ShapeDtypeStruct((bands, row_count, own), jnp.float32),
                jax.ShapeDtypeStruct((row_count, own), jnp.float32),
            ),
            in_specs=[vmem, vmem, vmem],
            out_specs=(hbm, vmem, vmem),
            scratch_shapes=[dma],
        )(*(pltpu.with_memory_space_constraint(x, pltpu.VMEM) for x in (smoothed, band, trans)))

    in_specs = (P("depth", "rows", None), P("depth", "rows", None), P(), P(), P())
    out_specs = (P("depth", "rows", None), P(None, "rows", "depth"), P("rows", "depth"))
    return jax.shard_map(body, mesh=mesh, in_specs=in_specs, out_specs=out_specs, check_vma=False)
```
